32 devices in a mesh: blk: 4 (over y, x), head: 8 (over z, core).
Axes of the slice: x: 2, y: 2, z: 4, core: 2. Of those that a mesh axis runs over, the one named last changes fastest.
Arguments:
- inputs: bfloat16 [4096, 2048], P(('blk', 'head')), may hold values from -6 to 6
- q_weight: float32 [2048, 2048], P('blk', 'head'), may hold values from -0.125 to 0.125
- k_weight: float32 [2048, 2048], P('blk', 'head'), may hold values from -0.125 to 0.125
- v_weight: float32 [2048, 2048], P('blk', 'head'), may hold values from -0.125 to 0.125
- o_weight: float32 [2048, 2048], P('blk', 'head'), may hold values from -1 to 1
- gate_weight: float32 [2048, 8192], P('blk', 'head'), may hold values from -0.125 to 0.125
- up_weight: float32 [2048, 8192], P('blk', 'head'), may hold values from -0.125 to 0.125
- down_weight: float32 [2048, 8192], P('blk', 'head'), may hold values from -0.0625 to 0.0625
- q_gain: float32 [128, 16], P(None, 'head'), may hold values from 0.5 to 1.5
- k_gain: float32 [128, 16], P(None, 'head'), may hold values from 0.5 to 1.5
- attn_gain: float32 [2048], replicated, may hold values from 0.5 to 1.5
- mlp_gain: float32 [2048], replicated, may hold values from 0.5 to 1.5
- block_ids: int32 [4096], replicated, may hold values from 0 to 20, never falling along the last dimension, each value on 1 to 256 neighbouring positions
- out_grad: bfloat16 [4096, 2048], P(('blk', 'head')), may hold values from -6 to 6
Outputs:
- output: bfloat16 [4096, 2048], P(('blk', 'head'))
- input_grad: bfloat16 [4096, 2048], P(('blk', 'head'))
- q_weight_grad: float32 [2048, 2048], P('blk', 'head')
- k_weight_grad: float32 [2048, 2048], P('blk', 'head')
- v_weight_grad: float32 [2048, 2048], P('blk', 'head')
- o_weight_grad: float32 [2048, 2048], P('blk', 'head')
- gate_weight_grad: float32 [2048, 8192], P('blk', 'head')
- up_weight_grad: float32 [2048, 8192], P('blk', 'head')
- down_weight_grad: float32 [2048, 8192], P('blk', 'head')
- q_gain_grad: float32 [128, 16], P('blk', 'head')
- k_gain_grad: float32 [128, 16], P('blk', 'head')
- attn_gain_grad: float32 [2048], P('blk')
- mlp_gain_grad: float32 [2048], P('blk')
The draws below stay inside these ranges and needn't reach their ends.
Inputs may be any that keep to these rules, and one draw needn't show every extreme that they name: `block_ids`: block ids never fall along the sequence; each block holds 1 to 256 tokens, one exactly 256.
All inputs are finite; a program needn't handle non-finite values.
Results may differ from the reference program's by a relative error of at most 0.029.
Values may be sent and summed in bfloat16 or wider, within the bound.
No kernel may reach another device: no remote copies, remote signals or barrier semaphores. Data moves between devices by JAX's collectives and lax.ppermute only.
A program may use at most 192 MiB of HBM per device.

```python
import math
import jax
import jax.numpy as jnp
import numpy as np
from jax import lax

D = 2048
HEADS = 16
HEAD_DIM = 128
FF = 8192
BLOCK = 256
TOKENS = 4096


def shard_levels(own_key, dims, cuts, smallest, high):
    def one(position, shards_of):
        draws = jax.random.uniform(jax.random.fold_in(jax.random.fold_in(own_key, 6), position), (shards_of,), jnp.float32, smallest / len(cuts), high / len(cuts))
        return jnp.repeat(jnp.exp(draws), dims[position] // shards_of).reshape((-1,) + (1,) * (len(dims) - position - 1))

    level = one(*cuts[0])
    for cut in cuts[1:]:
        level = level * one(*cut)
    return level


def length_profile(count, total, bound, skew):
    weights = [(1 << 20) // math.isqrt(rank ** skew) + 1 for rank in range(2, count + 1)]
    surplus, holding = total - bound - (count - 1), [1] * (count - 1)
    while surplus > 0:
        free = [i for i in range(count - 1) if holding[i] < bound]
        pool, remaining = sum([weights[i] for i in free]), surplus
        for i in free:
            extra = min(bound - holding[i], max(1, remaining * weights[i] // pool), surplus)
            holding[i] = holding[i] + extra
            surplus = surplus - extra
    return np.array([bound] + holding)


def ragged_sizes(key, amount, total, limit, skew):
    if amount == 2:
        one = jax.random.randint(key, (), max(1, total - limit), min(limit, total - 1) + 1)
        return jnp.stack([one, total - one])
    tallies = jnp.asarray(length_profile(amount, total, limit, skew), jnp.int32)
    couples = (amount - 1) // 2
    donor, sink = tallies[1:1 + 2 * couples:2], tallies[2:2 + 2 * couples:2]
    margin = jnp.minimum(donor - 1, limit - sink)
    moved = jax.random.randint(jax.random.fold_in(key, 1), (couples,), 0, 1 << 20) % (margin + 1)
    tallies = tallies.at[1:1 + 2 * couples:2].set(donor - moved).at[2:2 + 2 * couples:2].set(sink + moved)
    return tallies[jax.random.permutation(jax.random.fold_in(key, 2), amount)]


def gaussian(stream_key, extent, spread, limit, cuts=(), kind=jnp.bfloat16):
    entries = spread * jax.random.normal(stream_key, extent, jnp.float32)
    if cuts:
        entries = entries * shard_levels(stream_key, extent, cuts, -0.22, 0.18)
    return jnp.clip(entries, -limit, limit).astype(kind)


def setup_inputs(seed: int = 0) -> dict:
    arg_keys = jax.random.split(jax.random.key(seed), 15)
    inputs = gaussian(arg_keys[0], (TOKENS, D), 1.0, 6.0, ((0, 32),))
    q_weight = gaussian(arg_keys[1], (D, D), D ** -0.5, 0.125, ((0, 4), (1, 8)), jnp.float32)
    k_weight = gaussian(arg_keys[2], (D, D), D ** -0.5, 0.125, ((0, 4), (1, 8)), jnp.float32)
    v_weight = gaussian(arg_keys[3], (D, D), D ** -0.5, 0.125, ((0, 4), (1, 8)), jnp.float32)
    o_weight = gaussian(arg_keys[4], (D, D), (D // 64) ** -0.5, 1.0, ((0, 4), (1, 8)), jnp.float32)
    gate_weight = gaussian(arg_keys[5], (D, FF), D ** -0.5, 0.125, ((0, 4), (1, 8)), jnp.float32)
    up_weight = gaussian(arg_keys[6], (D, FF), D ** -0.5, 0.125, ((0, 4), (1, 8)), jnp.float32)
    down_weight = gaussian(arg_keys[7], (D, FF), FF ** -0.5, 0.0625, ((0, 4), (1, 8)), jnp.float32)
    q_gain = jnp.clip(1.0 + 0.1 * jax.random.normal(arg_keys[8], (HEAD_DIM, HEADS), jnp.float32), 0.5, 1.5)
    k_gain = jnp.clip(1.0 + 0.1 * jax.random.normal(arg_keys[9], (HEAD_DIM, HEADS), jnp.float32), 0.5, 1.5)
    attn_gain = jnp.clip(1.0 + 0.1 * jax.random.normal(arg_keys[10], (D,), jnp.float32), 0.5, 1.5)
    mlp_gain = jnp.clip(1.0 + 0.1 * jax.random.normal(arg_keys[11], (D,), jnp.float32), 0.5, 1.5)
    block_ids = jnp.searchsorted(jnp.cumsum(ragged_sizes(arg_keys[12], 4 * TOKENS // (3 * BLOCK), TOKENS, BLOCK, 0)), jnp.arange(TOKENS), side="right").astype(jnp.int32)
    out_grad = gaussian(arg_keys[13], (TOKENS, D), 1.0, 6.0, ((0, 32),))
    return {"inputs": inputs, "q_weight": q_weight, "k_weight": k_weight, "v_weight": v_weight, "o_weight": o_weight, "gate_weight": gate_weight, "up_weight": up_weight, "down_weight": down_weight, "q_gain": q_gain, "k_gain": k_gain, "attn_gain": attn_gain, "mlp_gain": mlp_gain, "block_ids": block_ids, "out_grad": out_grad}


@jax.custom_vjp
def low(v):
    return lax.optimization_barrier(v.astype(jnp.bfloat16)).astype(jnp.float32)

@jax.custom_vjp
def low_back(v):
    return v

def low_keep(v):
    return (low(v), None)

def low_pass(kept, grad):
    return (grad,)

def back_keep(v):
    return (v, None)

def back_low(kept, grad):
    return (low(grad),)
low.defvjp(low_keep, low_pass)
low_back.defvjp(back_keep, back_low)
epsilon = 1e-06
rope_base = 500000.0
highest = lax.Precision.HIGHEST

def matmul(left, right):
    return jnp.dot(left, right, precision=highest, preferred_element_type=jnp.float32)

def normalize(values):
    return values * lax.rsqrt(lax.optimization_barrier(jnp.mean(values * values, axis=-1, keepdims=True)) + epsilon)

def rotate(values, cosine_table, sine_table):
    half_dim = HEAD_DIM // 2
    leading = values[..., :half_dim]
    trailing = values[..., half_dim:]
    cos_rows = cosine_table[:, None, :]
    sin_rows = sine_table[:, None, :]
    return jnp.concatenate([leading * cos_rows - trailing * sin_rows, trailing * cos_rows + leading * sin_rows], axis=-1)

def attention(queries, keys, values, block_ids):
    scaling = HEAD_DIM ** (-0.5)
    block_rows = math.gcd(TOKENS, 512)
    block_count = TOKENS // block_rows

    def query_block(pieces):
        query_rows, query_ids = pieces
        scores = jnp.einsum('qhd,khd->hqk', query_rows, keys, precision=highest) * scaling
        scores = low_back(scores)
        allowed = block_ids[None, None, :] <= query_ids[None, :, None]
        scores = jnp.where(allowed, scores, -1e+30)
        biggest = lax.optimization_barrier(jnp.max(scores, axis=-1, keepdims=True))
        weights = jnp.where(allowed, jnp.exp(scores - biggest), 0.0)
        weights = weights / lax.optimization_barrier(jnp.sum(weights, axis=-1, keepdims=True))
        weights = low(weights)
        return jnp.einsum('hqk,khd->qhd', weights, values, precision=highest)
    blocks = lax.map(jax.checkpoint(query_block), (queries.reshape(block_count, block_rows, HEADS, HEAD_DIM), block_ids.reshape(block_count, block_rows)))
    return blocks.reshape(TOKENS, D)

def forward(inputs, q_weight, k_weight, v_weight, o_weight, gate_weight, up_weight, down_weight, q_gain, k_gain, attn_gain, mlp_gain, block_ids):
    query_raw = low_back(matmul(inputs, low(q_weight)))
    key_raw = low_back(matmul(inputs, low(k_weight)))
    value_raw = low(low_back(matmul(inputs, low(v_weight))))
    query_norm = normalize(query_raw) * q_gain.T.reshape(D)
    key_norm = normalize(key_raw) * k_gain.T.reshape(D)
    frequency = rope_base ** (-(jnp.arange(HEAD_DIM // 2, dtype=jnp.float32) * 2.0) / HEAD_DIM)
    angles = jnp.arange(TOKENS, dtype=jnp.float32)[:, None] * frequency[None, :]
    cosine_table = jnp.cos(angles)
    sine_table = jnp.sin(angles)
    queries = low(rotate(query_norm.reshape(TOKENS, HEADS, HEAD_DIM), cosine_table, sine_table))
    keys = low(rotate(key_norm.reshape(TOKENS, HEADS, HEAD_DIM), cosine_table, sine_table))
    values = value_raw.reshape(TOKENS, HEADS, HEAD_DIM)
    mixed = low(low_back(attention(queries, keys, values, block_ids)))
    attn_pre = low_back(matmul(mixed, low(o_weight).T))
    hidden = inputs + normalize(attn_pre) * attn_gain
    hidden_low = low(hidden)
    gate_pre = low_back(matmul(hidden_low, low(gate_weight)))
    up_pre = low_back(matmul(hidden_low, low(up_weight)))
    act = low(jax.nn.silu(gate_pre) * up_pre)
    mlp_pre = low_back(matmul(act, low(down_weight).T))
    return hidden + normalize(mlp_pre) * mlp_gain

def reference(inputs, q_weight, k_weight, v_weight, o_weight, gate_weight, up_weight, down_weight, q_gain, k_gain, attn_gain, mlp_gain, block_ids, out_grad):
    primals = (inputs.astype(jnp.float32), q_weight, k_weight, v_weight, o_weight, gate_weight, up_weight, down_weight, q_gain, k_gain, attn_gain, mlp_gain)

    def closed(*pieces):
        return forward(*pieces, block_ids)
    output, pullback = jax.vjp(closed, *primals)
    gradients = pullback(out_grad.astype(jnp.float32))
    return (output.astype(jnp.bfloat16), gradients[0].astype(jnp.bfloat16), gradients[1], gradients[2], gradients[3], gradients[4], gradients[5], gradients[6], gradients[7], gradients[8], gradients[9], gradients[10], gradients[11])
```

```python
import functools
import math

import jax
import jax.numpy as jnp
import numpy as np
from jax import lax
from jax.experimental import pallas as pl
from jax.experimental.pallas import tpu as pltpu
from jax.sharding import PartitionSpec as P


epsilon = 1e-06
rope_base = 500000.0
masked_score = -1e30
low = jnp.bfloat16
full = jnp.float32
vmem_limit = 60 * 1024 * 1024


def product(left, right):
    return jnp.dot(left, right, preferred_element_type=full)


def times_transposed(left, right):
    return lax.dot_general(left, right, (((1,), (1,)), ((), ())), preferred_element_type=full)


def transposed_times(left, right):
    return lax.dot_general(left, right, (((0,), (0,)), ((), ())), preferred_element_type=full)


def normalize(values):
    scaling = lax.rsqrt(jnp.mean(values * values, axis=1, keepdims=True) + epsilon)
    return (values * scaling, scaling)


def norm_back(hat_grad, hat_values, scaling):
    return scaling * (
        hat_grad - hat_values * jnp.mean(hat_grad * hat_values, axis=1, keepdims=True)
    )


class Rings:
    def __init__(self, count):
        self.count = count
        self.chips = count // 2
        order = list(range(0, self.chips, 2)) + list(range(1, self.chips, 2))[::-1]
        place = {chip: i for i, chip in enumerate(order)}
        self.back = np.array(
            [[order[(place[z] - j) % self.chips] for j in range(self.chips)] for z in range(self.chips)],
            dtype=np.int32,
        )
        nxt = {z: order[(place[z] + 1) % self.chips] for z in range(self.chips)}
        self.ring = [(2 * z + c, 2 * nxt[z] + c) for z in range(self.chips) for c in range(2)]
        self.swap = [(i, i ^ 1) for i in range(count)]

    def order(self):
        index = lax.axis_index("head")
        chips = jnp.asarray(self.back)[index // 2]
        cores = jnp.stack([index % 2, 1 - index % 2])
        return (2 * chips[:, None] + cores[None, :]).reshape(self.count).astype(jnp.int32)

    def swapped(self, values):
        return lax.ppermute(values, "head", self.swap)

    def onward(self, values):
        return lax.ppermute(values, "head", self.ring)

    def gather(self, values):
        chunks = []
        for step in range(self.chips):
            chunks.append(jnp.concatenate([values, self.swapped(values)], axis=0))
            if step + 1 < self.chips:
                values = self.onward(values)
        return chunks

    def scatter(self, partials):
        rows = partials[0].shape[0] // 2
        running = None
        for step in list(range(1, self.chips)) + [0]:
            part = partials[step]
            total = part[:rows].astype(full) + self.swapped(part[rows:]).astype(full)
            if running is not None:
                total = total + running.astype(full)
            if step == 0:
                return total
            running = self.onward(total.astype(low))
        return total


def head_sum(values):
    count = lax.axis_size("head")
    bit = 1
    while bit < count:
        values = values + lax.ppermute(values, "head", [(i, i ^ bit) for i in range(count)])
        bit *= 2
    return values


def blk_sum(values):
    count = lax.axis_size("blk")
    bit = 1
    while bit < count:
        values = values + lax.ppermute(values, "blk", [(i, i ^ bit) for i in range(count)])
        bit *= 2
    return values


def blk_pass(values, k):
    count = lax.axis_size("blk")
    return lax.ppermute(values, "blk", [(i, i ^ k) for i in range(count)])


def blk_gather(values):
    count = lax.axis_size("blk")
    if count != 4:
        return [values] + [blk_pass(values, k) for k in range(1, count)]
    half = values.shape[0] // 2
    along_x = blk_pass(values, 1)
    along_y = blk_pass(values, 2)
    upper = blk_pass(along_x[:half], 2)
    lower = blk_pass(along_y[half:], 1)
    return [values, along_x, along_y, jnp.concatenate([upper, lower], axis=0)]


def blk_scatter(parts):
    count = len(parts)
    if count != 4:
        total = parts[0].astype(full)
        for k in range(1, count):
            total = total + blk_pass(parts[k], k).astype(full)
        return total
    half = parts[0].shape[0] // 2
    upper = blk_pass(parts[3][:half], 1)
    lower = blk_pass(parts[3][half:], 2)
    for_y = jnp.concatenate(
        [(parts[2][:half].astype(full) + upper.astype(full)).astype(low), parts[2][half:]], axis=0
    )
    for_x = jnp.concatenate(
        [parts[1][:half], (parts[1][half:].astype(full) + lower.astype(full)).astype(low)], axis=0
    )
    return (
        parts[0].astype(full) + blk_pass(for_x, 1).astype(full) + blk_pass(for_y, 2).astype(full)
    )


def relative_columns(values):
    count = lax.axis_size("blk")
    index = lax.axis_index("blk")
    size = values.shape[1] // count
    return jnp.concatenate(
        [
            lax.dynamic_slice_in_dim(values, (index ^ k) * size, size, axis=1)
            for k in range(count)
        ],
        axis=1,
    )


def prepare_body(raw_ref, scale_ref, gain_ref, cos_ref, sin_ref, q_ref, k_ref, *, heads, dim, q_factor):
    cos_rows = cos_ref[...]
    sin_rows = sin_ref[...]
    for part, out_ref, factor in ((0, q_ref, q_factor), (1, k_ref, 1.0)):
        scale = scale_ref[:, part : part + 1] * factor
        for h in range(heads):
            at = (part * heads + h) * dim
            value = raw_ref[:, at : at + dim] * scale * gain_ref[0:1, at : at + dim]
            turned = value * cos_rows + pltpu.roll(value, dim // 2, 1) * sin_rows
            out_ref[:, h * dim : (h + 1) * dim] = turned.astype(low)


def prepare(raw, scale, gain, cos_table, sin_table, heads, dim, q_factor):
    rows = raw.shape[0]
    tile = min(rows, 512)
    width = heads * dim
    return pl.pallas_call(
        functools.partial(prepare_body, heads=heads, dim=dim, q_factor=q_factor),
        grid=(rows // tile,),
        in_specs=[
            pl.BlockSpec((tile, 2 * width), lambda i: (i, 0)),
            pl.BlockSpec((tile, 2), lambda i: (i, 0)),
            pl.BlockSpec((8, 2 * width), lambda i: (0, 0)),
            pl.BlockSpec((tile, dim), lambda i: (i, 0)),
            pl.BlockSpec((tile, dim), lambda i: (i, 0)),
        ],
        out_specs=[pl.BlockSpec((tile, width), lambda i: (i, 0))] * 2,
        out_shape=[jax.ShapeDtypeStruct((rows, width), low)] * 2,
        name="prepare",
        cost_estimate=pl.CostEstimate(
            flops=rows * width * 12, bytes_accessed=rows * width * 16, transcendentals=0
        ),
    )(raw, scale, gain, cos_table, sin_table)


def unrotate_body(grad_ref, cos_ref, sin_ref, out_ref, *, heads, dim):
    cos_rows = cos_ref[...]
    sin_rows = sin_ref[...]
    for h in range(heads):
        value = grad_ref[:, h * dim : (h + 1) * dim]
        out_ref[:, h * dim : (h + 1) * dim] = (
            value * cos_rows - pltpu.roll(value, dim // 2, 1) * sin_rows
        )


def unrotate(grads, cos_table, sin_table, heads, dim):
    rows = grads.shape[0]
    tile = min(rows, 512)
    width = heads * dim
    return pl.pallas_call(
        functools.partial(unrotate_body, heads=heads, dim=dim),
        grid=(rows // tile,),
        in_specs=[
            pl.BlockSpec((tile, width), lambda i: (i, 0)),
            pl.BlockSpec((tile, dim), lambda i: (i, 0)),
            pl.BlockSpec((tile, dim), lambda i: (i, 0)),
        ],
        out_specs=pl.BlockSpec((tile, width), lambda i: (i, 0)),
        out_shape=jax.ShapeDtypeStruct((rows, width), full),
        name="unrotate",
        cost_estimate=pl.CostEstimate(
            flops=rows * width * 4, bytes_accessed=rows * width * 8, transcendentals=0
        ),
    )(grads, cos_table, sin_table)


def over_keys(step, q_index, limits, ranges, tiles, key_tile):
    q_low, q_high, k_low, k_high = limits
    low_id = q_low[q_index]
    high_id = q_high[q_index]
    for r in range(ranges):

        def one(t, unused, r=r):
            first = k_low[r * tiles + t]
            last = k_high[r * tiles + t]
            row = pl.multiple_of(t * key_tile, key_tile)

            @pl.when(last <= low_id)
            def _():
                step(r, row, False)

            @pl.when(jnp.logical_and(last > low_id, first <= high_id))
            def _():
                step(r, row, True)

            return unused

        lax.fori_loop(0, tiles, one, 0)


def attend_body(*refs, ranges, tiles, key_tile, key_rows):
    limits = refs[:4]
    q_ref, q_ids_ref, k_ids_ref = refs[4:7]
    k_refs = refs[7 : 7 + ranges]
    v_refs = refs[7 + ranges : 7 + 2 * ranges]
    out_ref, total_ref, max_ref, sum_ref, acc_ref = refs[7 + 2 * ranges :]
    max_ref[...] = jnp.full(max_ref.shape, masked_score, full)
    sum_ref[...] = jnp.zeros(sum_ref.shape, full)
    acc_ref[...] = jnp.zeros(acc_ref.shape, full)

    def step(r, row, masked):
        scores = times_transposed(k_refs[r][pl.ds(row, key_tile), :], q_ref[...])
        if masked:
            ids = k_ids_ref[pl.ds(pl.multiple_of(r * key_rows + row, key_tile), key_tile), :]
            scores = jnp.where(ids <= q_ids_ref[0:1, :], scores, masked_score)
        old_max = max_ref[0:1, :]
        new_max = jnp.maximum(old_max, jnp.max(scores, axis=0, keepdims=True))
        weights = jnp.exp2(scores - new_max)
        shrink = jnp.exp2(old_max - new_max)
        sum_ref[0:1, :] = sum_ref[0:1, :] * shrink + jnp.sum(weights, axis=0, keepdims=True)
        max_ref[0:1, :] = new_max
        acc_ref[...] = acc_ref[...] * shrink + transposed_times(
            v_refs[r][pl.ds(row, key_tile), :], weights.astype(low)
        )

    over_keys(step, pl.program_id(1), limits, ranges, tiles, key_tile)
    out_ref[...] = jnp.transpose(acc_ref[...] / sum_ref[0:1, :]).astype(low)
    total_ref[...] = jnp.broadcast_to(
        max_ref[0:1, :] + jnp.log2(sum_ref[0:1, :]), total_ref.shape
    )


def attend(queries, keys_values, q_ids, k_ids, limits, heads, dim, q_tile, key_tile):
    rows = queries.shape[0]
    ranges = len(keys_values)
    tiles = rows // key_tile
    body = functools.partial(
        attend_body, ranges=ranges, tiles=tiles, key_tile=key_tile, key_rows=rows
    )
    pairs = rows * rows * ranges * heads
    return pl.pallas_call(
        body,
        grid_spec=pltpu.PrefetchScalarGridSpec(
            num_scalar_prefetch=4,
            grid=(heads, rows // q_tile),
            in_specs=[
                pl.BlockSpec((q_tile, dim), lambda h, i, *_: (i, h)),
                pl.BlockSpec((8, q_tile), lambda h, i, *_: (0, i)),
                pl.BlockSpec((rows * ranges, 1), lambda h, i, *_: (0, 0)),
            ]
            + [pl.BlockSpec((rows, dim), lambda h, i, *_: (0, h))] * ranges
            + [pl.BlockSpec((rows, dim), lambda h, i, *_: (0, heads + h))] * ranges,
            out_specs=[
                pl.BlockSpec((q_tile, dim), lambda h, i, *_: (i, h)),
                pl.BlockSpec((8, q_tile), lambda h, i, *_: (h, i)),
            ],
            scratch_shapes=[
                pltpu.VMEM((8, q_tile), full),
                pltpu.VMEM((8, q_tile), full),
                pltpu.VMEM((dim, q_tile), full),
            ],
        ),
        out_shape=[
            jax.ShapeDtypeStruct((rows, heads * dim), low),
            jax.ShapeDtypeStruct((8 * heads, rows), full),
        ],
        compiler_params=pltpu.CompilerParams(vmem_limit_bytes=vmem_limit),
        name="attend",
        cost_estimate=pl.CostEstimate(
            flops=pairs * dim * 4, bytes_accessed=rows * ranges * heads * dim * 4, transcendentals=pairs
        ),
    )(*limits, queries, q_ids, k_ids, *keys_values, *keys_values)


def attend_back_body(*refs, ranges, tiles, key_tile, key_rows, heads, dim):
    limits = refs[:4]
    q_ref, q_ids_ref, k_ids_ref, total_ref, grad_ref, mixed_ref, cos_ref, sin_ref = refs[4:12]
    k_refs = refs[12 : 12 + ranges]
    v_refs = refs[12 + ranges : 12 + 2 * ranges]
    q_out = refs[12 + 2 * ranges]
    kv_out = refs[13 + 2 * ranges : 13 + 3 * ranges]
    k_acc, v_acc, q_acc = refs[13 + 3 * ranges :]
    head = pl.program_id(0)
    q_index = pl.program_id(1)

    @pl.when(q_index == 0)
    def _():
        k_acc[...] = jnp.zeros(k_acc.shape, full)
        v_acc[...] = jnp.zeros(v_acc.shape, full)

    q_acc[...] = jnp.zeros(q_acc.shape, full)
    overlap = grad_ref[...].astype(full) * mixed_ref[...].astype(full)
    delta = jnp.sum(jnp.transpose(overlap), axis=0, keepdims=True)

    def step(r, row, masked):
        at = pl.multiple_of(r * key_rows + row, key_tile)
        k_tile = k_refs[r][pl.ds(row, key_tile), :]
        scores = times_transposed(k_tile, q_ref[...])
        probs = jnp.exp2(scores - total_ref[0:1, :])
        if masked:
            ids = k_ids_ref[pl.ds(at, key_tile), :]
            probs = jnp.where(ids <= q_ids_ref[0:1, :], probs, 0.0)
        prob_grad = times_transposed(v_refs[r][pl.ds(row, key_tile), :], grad_ref[...])
        score_grad = (probs * (prob_grad - delta)).astype(low)
        v_acc[pl.ds(at, key_tile), :] += product(probs.astype(low), grad_ref[...])
        k_acc[pl.ds(at, key_tile), :] += product(score_grad, q_ref[...])
        q_acc[...] += transposed_times(score_grad, k_tile)

    over_keys(step, q_index, limits, ranges, tiles, key_tile)
    q_grad = q_acc[...] * (dim**-0.5)
    q_out[...] = q_grad * cos_ref[...] - pltpu.roll(q_grad, dim // 2, 1) * sin_ref[...]

    @pl.when(q_index == pl.num_programs(1) - 1)
    def _():
        k_at = pl.multiple_of(head * dim, dim)
        v_at = pl.multiple_of((heads + head) * dim, dim)
        for r in range(ranges):
            rows = pl.ds(r * key_rows, key_rows)
            kv_out[r][:, pl.ds(k_at, dim)] = (k_acc[rows, :] * math.log(2.0)).astype(low)
            kv_out[r][:, pl.ds(v_at, dim)] = v_acc[rows, :].astype(low)


def attend_back(
    queries, keys_values, q_ids, k_ids, limits, totals, grads, mixed, cos_table, sin_table, heads, dim, q_tile, key_tile
):
    rows = queries.shape[0]
    ranges = len(keys_values)
    tiles = rows // key_tile
    body = functools.partial(
        attend_back_body,
        ranges=ranges,
        tiles=tiles,
        key_tile=key_tile,
        key_rows=rows,
        heads=heads,
        dim=dim,
    )
    pairs = rows * rows * ranges * heads
    return pl.pallas_call(
        body,
        grid_spec=pltpu.PrefetchScalarGridSpec(
            num_scalar_prefetch=4,
            grid=(heads, rows // q_tile),
            in_specs=[
                pl.BlockSpec((q_tile, dim), lambda h, i, *_: (i, h)),
                pl.BlockSpec((8, q_tile), lambda h, i, *_: (0, i)),
                pl.BlockSpec((rows * ranges, 1), lambda h, i, *_: (0, 0)),
                pl.BlockSpec((8, q_tile), lambda h, i, *_: (h, i)),
                pl.BlockSpec((q_tile, dim), lambda h, i, *_: (i, h)),
                pl.BlockSpec((q_tile, dim), lambda h, i, *_: (i, h)),
                pl.BlockSpec((q_tile, dim), lambda h, i, *_: (i, 0)),
                pl.BlockSpec((q_tile, dim), lambda h, i, *_: (i, 0)),
            ]
            + [pl.BlockSpec((rows, dim), lambda h, i, *_: (0, h))] * ranges
            + [pl.BlockSpec((rows, dim), lambda h, i, *_: (0, heads + h))] * ranges,
            out_specs=[pl.BlockSpec((q_tile, dim), lambda h, i, *_: (i, h))]
            + [pl.BlockSpec((rows, 2 * heads * dim), lambda h, i, *_: (0, 0))] * ranges,
            scratch_shapes=[
                pltpu.VMEM((rows * ranges, dim), full),
                pltpu.VMEM((rows * ranges, dim), full),
                pltpu.VMEM((q_tile, dim), full),
            ],
        ),
        out_shape=[jax.ShapeDtypeStruct((rows, heads * dim), full)]
        + [jax.ShapeDtypeStruct((rows, 2 * heads * dim), low)] * ranges,
        compiler_params=pltpu.CompilerParams(vmem_limit_bytes=vmem_limit),
        name="attend_back",
        cost_estimate=pl.CostEstimate(
            flops=pairs * dim * 10,
            bytes_accessed=rows * ranges * heads * dim * 8,
            transcendentals=pairs,
        ),
    )(*limits, queries, q_ids, k_ids, totals, grads, mixed, cos_table, sin_table, *keys_values, *keys_values)


def local(
    inputs,
    q_weight,
    k_weight,
    v_weight,
    o_weight,
    gate_weight,
    up_weight,
    down_weight,
    q_gain,
    k_gain,
    attn_gain,
    mlp_gain,
    block_ids,
    out_grad,
):
    groups = lax.axis_size("head")
    ranges = lax.axis_size("blk")
    range_index = lax.axis_index("blk")
    rings = Rings(groups)
    tok_rows = inputs.shape[0]
    rows_all = tok_rows * groups
    width = inputs.shape[1]
    cols = q_weight.shape[1]
    dim = q_gain.shape[0]
    heads = cols // dim
    slab = width // ranges
    q_tile = math.gcd(rows_all, 512)
    key_tile = math.gcd(rows_all, 512)

    gate_full, up_full, down_full = (
        lax.all_gather(w.astype(low), "blk", axis=0, tiled=True)
        for w in (gate_weight, up_weight, down_weight)
    )
    qkv_own = jnp.concatenate([q_weight, k_weight, v_weight], axis=1).astype(low)
    qkv_full = jnp.concatenate(blk_gather(qkv_own), axis=0)
    rows_chunks = rings.gather(relative_columns(inputs))
    rows_in = jnp.concatenate(rows_chunks, axis=0)
    output_full = jnp.concatenate(blk_gather(o_weight.astype(low)), axis=0)

    order = rings.order()
    token_rows = jnp.arange(tok_rows, dtype=jnp.int32)
    positions = ((range_index * groups + order)[:, None] * tok_rows + token_rows[None, :]).reshape(-1)
    frequency = rope_base ** (-(jnp.arange(dim // 2, dtype=full) * 2.0) / dim)
    angles = positions.astype(full)[:, None] * frequency[None, :]
    cosine, sine = (jnp.cos(angles), jnp.sin(angles))
    cos_table = jnp.concatenate([cosine, cosine], axis=1)
    sin_table = jnp.concatenate([-sine, sine], axis=1)
    id_rows = block_ids.reshape(ranges * groups, tok_rows)
    relative = range_index ^ jnp.arange(ranges, dtype=jnp.int32)
    key_ids = id_rows[(relative[:, None] * groups + order[None, :]).reshape(-1)].reshape(-1)
    query_ids = key_ids[:rows_all]
    q_ids = jnp.broadcast_to(query_ids[None, :], (8, rows_all))
    k_ids = key_ids[:, None]
    limits = (
        jnp.min(query_ids.reshape(-1, q_tile), axis=1),
        jnp.max(query_ids.reshape(-1, q_tile), axis=1),
        jnp.min(key_ids.reshape(-1, key_tile), axis=1),
        jnp.max(key_ids.reshape(-1, key_tile), axis=1),
    )

    qk_raw = product(rows_in, qkv_full[:, : 2 * cols])
    squares = jnp.stack(
        [jnp.sum(qk_raw[:, i * cols : (i + 1) * cols] ** 2, axis=1) for i in range(2)]
    ).reshape(2, groups, tok_rows)
    placing = (order[None, :] == jnp.arange(groups)[:, None]).astype(full)
    in_true_order = jnp.sum(placing[None, :, :, None] * squares[:, None], axis=2)
    summed = head_sum(in_true_order)
    squares = jnp.sum(placing[None, :, :, None] * summed[:, :, None], axis=1).reshape(2, rows_all)
    scales = lax.rsqrt(squares / width + epsilon).T
    value_raw = product(rows_in, qkv_full[:, 2 * cols :]).astype(low)
    gain_cols = jnp.concatenate([q_gain.T.reshape(cols), k_gain.T.reshape(cols)])
    q_factor = dim**-0.5 / math.log(2.0)
    query_rot, key_rot = prepare(
        qk_raw,
        scales,
        jnp.broadcast_to(gain_cols[None, :], (8, 2 * cols)),
        cos_table,
        sin_table,
        heads,
        dim,
        q_factor,
    )
    keys_values = blk_gather(jnp.concatenate([key_rot, value_raw], axis=1))
    mixed_low, totals = attend(
        query_rot, keys_values, q_ids, k_ids, limits, heads, dim, q_tile, key_tile
    )

    attn_own = relative_columns(
        rings.scatter(
            [
                times_transposed(mixed_low[j * 2 * tok_rows : (j + 1) * 2 * tok_rows], output_full).astype(low)
                for j in range(rings.chips)
            ]
        )
    )
    attn_hat, attn_scale = normalize(attn_own)
    hidden = inputs.astype(full) + attn_hat * attn_gain

    mid_chunks = rings.gather(hidden.astype(low))
    gates, ups, acts, parts = ([], [], [], [])
    for chunk in mid_chunks:
        gate_pre = product(chunk, gate_full)
        up_pre = product(chunk, up_full)
        act = (gate_pre * jax.nn.sigmoid(gate_pre) * up_pre).astype(low)
        gates.append(gate_pre)
        ups.append(up_pre)
        acts.append(act)
        parts.append(times_transposed(act, down_full).astype(low))
    mlp_own = rings.scatter(parts)
    mlp_hat, mlp_scale = normalize(mlp_own)
    result = (hidden + mlp_hat * mlp_gain).astype(low)
    grad_out = out_grad.astype(full)
    mlp_gain_part = jnp.sum(grad_out * mlp_hat, axis=0)
    mlp_grad = norm_back(grad_out * mlp_gain, mlp_hat, mlp_scale).astype(low)

    grad_chunks = rings.gather(mlp_grad)
    gate_grads, up_grads, parts = ([], [], [])
    for chunk, gate_pre, up_pre in zip(grad_chunks, gates, ups):
        act_grad = product(chunk, down_full)
        sigmoid_gate = jax.nn.sigmoid(gate_pre)
        gate_grad = (
            act_grad * up_pre * sigmoid_gate * (1.0 + gate_pre * (1.0 - sigmoid_gate))
        ).astype(low)
        up_grad = (act_grad * gate_pre * sigmoid_gate).astype(low)
        gate_grads.append(gate_grad)
        up_grads.append(up_grad)
        parts.append(
            (times_transposed(gate_grad, gate_full) + times_transposed(up_grad, up_full)).astype(low)
        )
    hidden_grad = grad_out + rings.scatter(parts)
    rows_mid = jnp.concatenate(mid_chunks, axis=0)
    down_term = transposed_times(
        jnp.concatenate(grad_chunks, axis=0), jnp.concatenate(acts, axis=0)
    )
    gate_term = transposed_times(rows_mid, jnp.concatenate(gate_grads, axis=0))
    up_term = transposed_times(rows_mid, jnp.concatenate(up_grads, axis=0))
    down_sum, gate_sum, up_sum = (
        lax.psum_scatter(term.astype(low), "blk", scatter_dimension=0, tiled=True).astype(full)
        for term in (down_term, gate_term, up_term)
    )
    attn_gain_part = jnp.sum(hidden_grad * attn_hat, axis=0)
    attn_grad = norm_back(hidden_grad * attn_gain, attn_hat, attn_scale).astype(low)
    gain_sums = head_sum(jnp.concatenate([attn_gain_part, mlp_gain_part]).reshape(-1, 128))

    attn_grad_chunks = rings.gather(relative_columns(attn_grad))
    mixed_grad = jnp.concatenate(
        [product(chunk, output_full).astype(low) for chunk in attn_grad_chunks], axis=0
    )
    attn_grad_rows = jnp.concatenate(attn_grad_chunks, axis=0)
    output_sum = blk_scatter(
        [
            transposed_times(attn_grad_rows[:, k * slab : (k + 1) * slab], mixed_low).astype(low)
            for k in range(ranges)
        ]
    )
    query_norm_grad, *kv_parts = attend_back(
        query_rot,
        keys_values,
        q_ids,
        k_ids,
        limits,
        totals,
        mixed_grad,
        mixed_low,
        cos_table,
        sin_table,
        heads,
        dim,
        q_tile,
        key_tile,
    )

    def norm_sums(norm_grad, raw, scale, gains):
        weighted = norm_grad * gains
        return (
            weighted,
            jnp.sum(weighted * raw, axis=1),
            jnp.sum(norm_grad * raw * scale, axis=0),
        )

    def over_heads(dots):
        ordered = jnp.sum(placing[:, :, None] * dots.reshape(1, groups, tok_rows), axis=1)
        total = head_sum(ordered)
        return jnp.sum(placing[:, :, None] * total[:, None], axis=0).reshape(rows_all, 1)

    query_raw, key_raw = (qk_raw[:, :cols], qk_raw[:, cols:])
    query_scale, key_scale = (scales[:, 0:1], scales[:, 1:2])
    query_weighted, query_dots, query_gain_part = norm_sums(
        query_norm_grad, query_raw, query_scale, gain_cols[:cols]
    )
    query_dot = over_heads(query_dots)
    kv_grad = blk_scatter(kv_parts)
    value_raw_grad = kv_grad[:, cols:].astype(low)
    key_norm_grad = unrotate(kv_grad[:, :cols], cos_table, sin_table, heads, dim)
    key_weighted, key_dots, key_gain_part = norm_sums(
        key_norm_grad, key_raw, key_scale, gain_cols[cols:]
    )
    key_dot = over_heads(key_dots)
    query_raw_grad = (
        query_scale * query_weighted - query_raw * (query_scale**3 * query_dot / width)
    ).astype(low)
    key_raw_grad = (
        key_scale * key_weighted - key_raw * (key_scale**3 * key_dot / width)
    ).astype(low)
    raw_grads = jnp.concatenate([query_raw_grad, key_raw_grad, value_raw_grad], axis=1)
    input_grad = (
        hidden_grad
        + relative_columns(
            rings.scatter(
                [
                    times_transposed(
                        raw_grads[j * 2 * tok_rows : (j + 1) * 2 * tok_rows], qkv_full
                    ).astype(low)
                    for j in range(rings.chips)
                ]
            )
        )
    ).astype(low)
    qkv_sum = blk_scatter(
        [
            transposed_times(rows_in[:, k * slab : (k + 1) * slab], raw_grads).astype(low)
            for k in range(ranges)
        ]
    )
    small = blk_sum(
        jnp.concatenate(
            [gain_sums, query_gain_part.reshape(heads, dim), key_gain_part.reshape(heads, dim)], axis=0
        )
        if dim == 128
        else None
    )
    gain_rows = width // 128
    gain_at = range_index * (width // ranges)
    attn_gain_grad = lax.dynamic_slice_in_dim(
        small[:gain_rows].reshape(width), gain_at, width // ranges
    )
    mlp_gain_grad = lax.dynamic_slice_in_dim(
        small[gain_rows : 2 * gain_rows].reshape(width), gain_at, width // ranges
    )
    piece = dim // ranges
    q_gain_grad, k_gain_grad = (
        lax.dynamic_slice_in_dim(
            small[2 * gain_rows + i * heads : 2 * gain_rows + (i + 1) * heads].T,
            range_index * piece,
            piece,
        )
        for i in range(2)
    )
    return (
        result,
        input_grad,
        qkv_sum[:, :cols],
        qkv_sum[:, cols : 2 * cols],
        qkv_sum[:, 2 * cols :],
        output_sum,
        gate_sum,
        up_sum,
        down_sum,
        q_gain_grad,
        k_gain_grad,
        attn_gain_grad,
        mlp_gain_grad,
    )


def solution(mesh):
    in_specs = (
        P(("blk", "head"), None),
        P("blk", "head"),
        P("blk", "head"),
        P("blk", "head"),
        P("blk", "head"),
        P("blk", "head"),
        P("blk", "head"),
        P("blk", "head"),
        P(None, "head"),
        P(None, "head"),
        P(),
        P(),
        P(),
        P(("blk", "head"), None),
    )
    out_specs = (
        P(("blk", "head"), None),
        P(("blk", "head"), None),
        P("blk", "head"),
        P("blk", "head"),
        P("blk", "head"),
        P("blk", "head"),
        P("blk", "head"),
        P("blk", "head"),
        P("blk", "head"),
        P("blk", "head"),
        P("blk", "head"),
        P("blk"),
        P("blk"),
    )
    return jax.shard_map(local, mesh=mesh, in_specs=in_specs, out_specs=out_specs, check_vma=False)
```

```python
import functools
import math

import jax
import jax.numpy as jnp
import numpy as np
from jax import lax
from jax.experimental import pallas as pl
from jax.experimental.pallas import tpu as pltpu
from jax.sharding import PartitionSpec as P


epsilon = 1e-06
rope_base = 500000.0
masked_score = -1e30
low = jnp.bfloat16
full = jnp.float32
vmem_limit = 60 * 1024 * 1024


def product(left, right):
    return jnp.dot(left, right, preferred_element_type=full)


def times_transposed(left, right):
    return lax.dot_general(left, right, (((1,), (1,)), ((), ())), preferred_element_type=full)


def transposed_times(left, right):
    return lax.dot_general(left, right, (((0,), (0,)), ((), ())), preferred_element_type=full)


def normalize(values):
    scaling = lax.rsqrt(jnp.mean(values * values, axis=1, keepdims=True) + epsilon)
    return (values * scaling, scaling)


def norm_back(hat_grad, hat_values, scaling):
    return scaling * (
        hat_grad - hat_values * jnp.mean(hat_grad * hat_values, axis=1, keepdims=True)
    )


class Rings:
    def __init__(self, count):
        self.count = count
        self.chips = count // 2
        order = list(range(0, self.chips, 2)) + list(range(1, self.chips, 2))[::-1]
        place = {chip: i for i, chip in enumerate(order)}
        self.back = np.array(
            [[order[(place[z] - j) % self.chips] for j in range(self.chips)] for z in range(self.chips)],
            dtype=np.int32,
        )
        nxt = {z: order[(place[z] + 1) % self.chips] for z in range(self.chips)}
        self.ring = [(2 * z + c, 2 * nxt[z] + c) for z in range(self.chips) for c in range(2)]
        self.swap = [(i, i ^ 1) for i in range(count)]

    def order(self):
        index = lax.axis_index("head")
        chips = jnp.asarray(self.back)[index // 2]
        cores = jnp.stack([index % 2, 1 - index % 2])
        return (2 * chips[:, None] + cores[None, :]).reshape(self.count).astype(jnp.int32)

    def swapped(self, values):
        return lax.ppermute(values, "head", self.swap)

    def onward(self, values):
        return lax.ppermute(values, "head", self.ring)

    def gather(self, values):
        chunks = []
        for step in range(self.chips):
            chunks.append(jnp.concatenate([values, self.swapped(values)], axis=0))
            if step + 1 < self.chips:
                values = self.onward(values)
        return chunks

    def scatter(self, partials):
        rows = partials[0].shape[0] // 2
        running = None
        for step in list(range(1, self.chips)) + [0]:
            part = partials[step]
            total = part[:rows].astype(full) + self.swapped(part[rows:]).astype(full)
            if running is not None:
                total = total + running.astype(full)
            if step == 0:
                return total
            running = self.onward(total.astype(low))
        return total


def head_sum(values):
    count = lax.axis_size("head")
    bit = 1
    while bit < count:
        values = values + lax.ppermute(values, "head", [(i, i ^ bit) for i in range(count)])
        bit *= 2
    return values


def blk_sum(values):
    count = lax.axis_size("blk")
    bit = 1
    while bit < count:
        values = values + lax.ppermute(values, "blk", [(i, i ^ bit) for i in range(count)])
        bit *= 2
    return values


def blk_pass(values, k):
    count = lax.axis_size("blk")
    return lax.ppermute(values, "blk", [(i, i ^ k) for i in range(count)])


def blk_gather(values):
    count = lax.axis_size("blk")
    if count != 4:
        return [values] + [blk_pass(values, k) for k in range(1, count)]
    half = values.shape[0] // 2
    along_x = blk_pass(values, 1)
    along_y = blk_pass(values, 2)
    upper = blk_pass(along_x[:half], 2)
    lower = blk_pass(along_y[half:], 1)
    return [values, along_x, along_y, jnp.concatenate([upper, lower], axis=0)]


def blk_gather_pair(first, second):
    count = lax.axis_size("blk")
    if count != 4:
        return tuple([v] + [blk_pass(v, k) for k in range(1, count)] for v in (first, second))
    first_x, first_y = (blk_pass(first, 1), blk_pass(first, 2))
    second_x, second_y = (blk_pass(second, 1), blk_pass(second, 2))
    return (
        [first, first_x, first_y, blk_pass(first_x, 2)],
        [second, second_x, second_y, blk_pass(second_y, 1)],
    )


def blk_scatter(part):
    count = lax.axis_size("blk")
    if count != 4:
        total = part(0)
        for k in range(1, count):
            total = total + blk_pass(part(k).astype(low), k).astype(full)
        return total
    corner = part(3).astype(low)
    half = corner.shape[0] // 2
    upper = blk_pass(corner[:half], 1)
    lower = blk_pass(corner[half:], 2)
    along_y, along_x = (part(2), part(1))
    for_y = jnp.concatenate([along_y[:half] + upper.astype(full), along_y[half:]], axis=0)
    for_x = jnp.concatenate([along_x[:half], along_x[half:] + lower.astype(full)], axis=0)
    return (
        part(0)
        + blk_pass(for_x.astype(low), 1).astype(full)
        + blk_pass(for_y.astype(low), 2).astype(full)
    )


def relative_columns(values):
    count = lax.axis_size("blk")
    index = lax.axis_index("blk")
    size = values.shape[1] // count
    return jnp.concatenate(
        [
            lax.dynamic_slice_in_dim(values, (index ^ k) * size, size, axis=1)
            for k in range(count)
        ],
        axis=1,
    )


def prepare_body(raw_ref, scale_ref, gain_ref, cos_ref, sin_ref, q_ref, k_ref, *, heads, dim, q_factor):
    cos_rows = cos_ref[...]
    sin_rows = sin_ref[...]
    for part, out_ref, factor in ((0, q_ref, q_factor), (1, k_ref, 1.0)):
        scale = scale_ref[:, part : part + 1] * factor
        for h in range(heads):
            at = (part * heads + h) * dim
            value = raw_ref[:, at : at + dim] * scale * gain_ref[0:1, at : at + dim]
            turned = value * cos_rows + pltpu.roll(value, dim // 2, 1) * sin_rows
            out_ref[:, h * dim : (h + 1) * dim] = turned.astype(low)


def prepare(raw, scale, gain, cos_table, sin_table, heads, dim, q_factor):
    rows = raw.shape[0]
    tile = min(rows, 512)
    width = heads * dim
    return pl.pallas_call(
        functools.partial(prepare_body, heads=heads, dim=dim, q_factor=q_factor),
        grid=(rows // tile,),
        in_specs=[
            pl.BlockSpec((tile, 2 * width), lambda i: (i, 0)),
            pl.BlockSpec((tile, 2), lambda i: (i, 0)),
            pl.BlockSpec((8, 2 * width), lambda i: (0, 0)),
            pl.BlockSpec((tile, dim), lambda i: (i, 0)),
            pl.BlockSpec((tile, dim), lambda i: (i, 0)),
        ],
        out_specs=[pl.BlockSpec((tile, width), lambda i: (i, 0))] * 2,
        out_shape=[jax.ShapeDtypeStruct((rows, width), low)] * 2,
        name="prepare",
        cost_estimate=pl.CostEstimate(
            flops=rows * width * 12, bytes_accessed=rows * width * 16, transcendentals=0
        ),
    )(raw, scale, gain, cos_table, sin_table)


def unrotate_body(grad_ref, cos_ref, sin_ref, out_ref):
    value = grad_ref[...]
    out_ref[...] = value * cos_ref[...] - pltpu.roll(value, value.shape[1] // 2, 1) * sin_ref[...]


def unrotate(grads, cos_table, sin_table):
    rows, dim = cos_table.shape
    spec = pl.BlockSpec((rows, dim), lambda i: (0, 0))
    return pl.pallas_call(
        unrotate_body,
        grid=(1,),
        in_specs=[spec, spec, spec],
        out_specs=spec,
        out_shape=jax.ShapeDtypeStruct((rows, dim), full),
        name="unrotate",
        cost_estimate=pl.CostEstimate(
            flops=rows * dim * 4, bytes_accessed=rows * dim * 16, transcendentals=0
        ),
    )(grads, cos_table, sin_table)


def over_keys(step, q_index, limits, ranges, tiles, key_tile):
    q_low, q_high, k_low, k_high = limits
    low_id = q_low[q_index]
    high_id = q_high[q_index]
    for r in range(ranges):

        def one(t, unused, r=r):
            first = k_low[r * tiles + t]
            last = k_high[r * tiles + t]
            row = pl.multiple_of(t * key_tile, key_tile)

            @pl.when(last <= low_id)
            def _():
                step(r, row, False)

            @pl.when(jnp.logical_and(last > low_id, first <= high_id))
            def _():
                step(r, row, True)

            return unused

        lax.fori_loop(0, tiles, one, 0)


def attend_body(*refs, ranges, tiles, key_tile, key_rows, heads, dim):
    limits = refs[:4]
    q_ref, q_ids_ref, k_ids_ref = refs[4:7]
    k_refs = refs[7 : 7 + ranges]
    v_refs = refs[7 + ranges : 7 + 2 * ranges]
    out_ref, total_ref, max_ref, sum_ref, acc_ref = refs[7 + 2 * ranges :]
    max_ref[...] = jnp.full(max_ref.shape, masked_score, full)
    sum_ref[...] = jnp.zeros(sum_ref.shape, full)
    acc_ref[...] = jnp.zeros(acc_ref.shape, full)

    def step(r, row, masked):
        rows = pl.ds(row, key_tile)
        scores = [
            times_transposed(
                k_refs[r][rows, h * dim : (h + 1) * dim], q_ref[:, h * dim : (h + 1) * dim]
            )
            for h in range(heads)
        ]
        if masked:
            ids = k_ids_ref[pl.ds(pl.multiple_of(r * key_rows + row, key_tile), key_tile), :]
            kept = ids <= q_ids_ref[0:1, :]
            scores = [jnp.where(kept, s, masked_score) for s in scores]
        for h in range(heads):
            at = slice(8 * h, 8 * h + 1)
            old_max = max_ref[at, :]
            new_max = jnp.maximum(old_max, jnp.max(scores[h], axis=0, keepdims=True))
            weights = jnp.exp2(scores[h] - new_max)
            shrink = jnp.exp2(old_max - new_max)
            sum_ref[at, :] = sum_ref[at, :] * shrink + jnp.sum(weights, axis=0, keepdims=True)
            max_ref[at, :] = new_max
            acc_ref[h] = acc_ref[h] * shrink + transposed_times(
                v_refs[r][rows, h * dim : (h + 1) * dim], weights.astype(low)
            )

    over_keys(step, pl.program_id(0), limits, ranges, tiles, key_tile)
    for h in range(heads):
        at = slice(8 * h, 8 * h + 1)
        out_ref[:, h * dim : (h + 1) * dim] = jnp.transpose(acc_ref[h] / sum_ref[at, :]).astype(low)
        total_ref[8 * h : 8 * h + 8, :] = jnp.broadcast_to(
            max_ref[at, :] + jnp.log2(sum_ref[at, :]), (8, max_ref.shape[1])
        )


def attend(queries, keys, values, q_ids, k_ids, limits, heads, dim, q_tile, key_tile):
    rows = queries.shape[0]
    ranges = len(keys)
    tiles = rows // key_tile
    body = functools.partial(
        attend_body,
        ranges=ranges,
        tiles=tiles,
        key_tile=key_tile,
        key_rows=rows,
        heads=heads,
        dim=dim,
    )
    pairs = rows * rows * ranges * heads
    return pl.pallas_call(
        body,
        grid_spec=pltpu.PrefetchScalarGridSpec(
            num_scalar_prefetch=4,
            grid=(rows // q_tile,),
            in_specs=[
                pl.BlockSpec((q_tile, heads * dim), lambda i, *_: (i, 0)),
                pl.BlockSpec((8, q_tile), lambda i, *_: (0, i)),
                pl.BlockSpec((rows * ranges, 1), lambda i, *_: (0, 0)),
            ]
            + [pl.BlockSpec((rows, heads * dim), lambda i, *_: (0, 0))] * (2 * ranges),
            out_specs=[
                pl.BlockSpec((q_tile, heads * dim), lambda i, *_: (i, 0)),
                pl.BlockSpec((8 * heads, q_tile), lambda i, *_: (0, i)),
            ],
            scratch_shapes=[
                pltpu.VMEM((8 * heads, q_tile), full),
                pltpu.VMEM((8 * heads, q_tile), full),
                pltpu.VMEM((heads, dim, q_tile), full),
            ],
        ),
        out_shape=[
            jax.ShapeDtypeStruct((rows, heads * dim), low),
            jax.ShapeDtypeStruct((8 * heads, rows), full),
        ],
        compiler_params=pltpu.CompilerParams(vmem_limit_bytes=vmem_limit),
        name="attend",
        cost_estimate=pl.CostEstimate(
            flops=pairs * dim * 4, bytes_accessed=rows * ranges * heads * dim * 4, transcendentals=pairs
        ),
    )(*limits, queries, q_ids, k_ids, *keys, *values)


def attend_back_body(*refs, ranges, tiles, key_tile, key_rows, dim):
    limits = refs[:4]
    q_ref, q_ids_ref, k_ids_ref, total_ref, grad_ref, mixed_ref, cos_ref, sin_ref = refs[4:12]
    k_refs = refs[12 : 12 + ranges]
    v_refs = refs[12 + ranges : 12 + 2 * ranges]
    q_out = refs[12 + 2 * ranges]
    kv_out = refs[13 + 2 * ranges : 13 + 3 * ranges]
    k_acc, v_acc, q_acc = refs[13 + 3 * ranges :]
    q_index = pl.program_id(0)

    @pl.when(q_index == 0)
    def _():
        k_acc[...] = jnp.zeros(k_acc.shape, full)
        v_acc[...] = jnp.zeros(v_acc.shape, full)

    q_acc[...] = jnp.zeros(q_acc.shape, full)
    overlap = grad_ref[...].astype(full) * mixed_ref[...].astype(full)
    delta = jnp.sum(jnp.transpose(overlap), axis=0, keepdims=True)

    def step(r, row, masked):
        at = pl.multiple_of(r * key_rows + row, key_tile)
        k_tile = k_refs[r][pl.ds(row, key_tile), :]
        scores = times_transposed(k_tile, q_ref[...])
        probs = jnp.exp2(scores - total_ref[0:1, :])
        if masked:
            ids = k_ids_ref[pl.ds(at, key_tile), :]
            probs = jnp.where(ids <= q_ids_ref[0:1, :], probs, 0.0)
        prob_grad = times_transposed(v_refs[r][pl.ds(row, key_tile), :], grad_ref[...])
        score_grad = (probs * (prob_grad - delta)).astype(low)
        v_acc[pl.ds(at, key_tile), :] += product(probs.astype(low), grad_ref[...])
        k_acc[pl.ds(at, key_tile), :] += product(score_grad, q_ref[...])
        q_acc[...] += transposed_times(score_grad, k_tile)

    over_keys(step, q_index, limits, ranges, tiles, key_tile)
    q_grad = q_acc[...] * (dim**-0.5)
    q_out[...] = q_grad * cos_ref[...] - pltpu.roll(q_grad, dim // 2, 1) * sin_ref[...]

    @pl.when(q_index == pl.num_programs(0) - 1)
    def _():
        for r in range(ranges):
            rows = pl.ds(r * key_rows, key_rows)
            kv_out[r][:, :dim] = (k_acc[rows, :] * math.log(2.0)).astype(low)
            kv_out[r][:, dim:] = v_acc[rows, :].astype(low)


def attend_back(
    head, queries, keys, values, q_ids, k_ids, limits, totals, grads, mixed, cos_table, sin_table, dim, q_tile, key_tile
):
    rows = queries.shape[0]
    ranges = len(keys)
    tiles = rows // key_tile
    body = functools.partial(
        attend_back_body, ranges=ranges, tiles=tiles, key_tile=key_tile, key_rows=rows, dim=dim
    )
    pairs = rows * rows * ranges
    own = pl.BlockSpec((q_tile, dim), lambda i, *_: (i, head))
    return pl.pallas_call(
        body,
        grid_spec=pltpu.PrefetchScalarGridSpec(
            num_scalar_prefetch=4,
            grid=(rows // q_tile,),
            in_specs=[
                own,
                pl.BlockSpec((8, q_tile), lambda i, *_: (0, i)),
                pl.BlockSpec((rows * ranges, 1), lambda i, *_: (0, 0)),
                pl.BlockSpec((8, q_tile), lambda i, *_: (head, i)),
                own,
                own,
                pl.BlockSpec((q_tile, dim), lambda i, *_: (i, 0)),
                pl.BlockSpec((q_tile, dim), lambda i, *_: (i, 0)),
            ]
            + [pl.BlockSpec((rows, dim), lambda i, *_: (0, head))] * (2 * ranges),
            out_specs=[pl.BlockSpec((q_tile, dim), lambda i, *_: (i, 0))]
            + [pl.BlockSpec((rows, 2 * dim), lambda i, *_: (0, 0))] * ranges,
            scratch_shapes=[
                pltpu.VMEM((rows * ranges, dim), full),
                pltpu.VMEM((rows * ranges, dim), full),
                pltpu.VMEM((q_tile, dim), full),
            ],
        ),
        out_shape=[jax.ShapeDtypeStruct((rows, dim), full)]
        + [jax.ShapeDtypeStruct((rows, 2 * dim), low)] * ranges,
        compiler_params=pltpu.CompilerParams(vmem_limit_bytes=vmem_limit),
        name="attend_back",
        cost_estimate=pl.CostEstimate(
            flops=pairs * dim * 10, bytes_accessed=rows * ranges * dim * 8, transcendentals=pairs
        ),
    )(*limits, queries, q_ids, k_ids, totals, grads, mixed, cos_table, sin_table, *keys, *values)


def layer(
    inputs,
    q_weight,
    k_weight,
    v_weight,
    o_weight,
    gate_weight,
    up_weight,
    down_weight,
    q_gain,
    k_gain,
    attn_gain,
    mlp_gain,
    block_ids,
    out_grad,
):
    groups = lax.axis_size("head")
    ranges = lax.axis_size("blk")
    range_index = lax.axis_index("blk")
    rings = Rings(groups)
    tok_rows = inputs.shape[0]
    rows_all = tok_rows * groups
    width = inputs.shape[1]
    cols = q_weight.shape[1]
    dim = q_gain.shape[0]
    heads = cols // dim
    slab = width // ranges
    q_tile = math.gcd(rows_all, 512)
    key_tile = math.gcd(rows_all, 512)
    wide_tile = math.gcd(rows_all, 1024)

    inputs = relative_columns(inputs)
    out_grad = relative_columns(out_grad)
    attn_gain, mlp_gain = relative_columns(jnp.stack([attn_gain, mlp_gain]))
    qkv_full = jnp.concatenate(
        blk_gather(jnp.concatenate([q_weight, k_weight, v_weight], axis=1).astype(low)), axis=0
    )
    output_full, gate_full, up_full, down_full = (
        jnp.concatenate(blk_gather(weight.astype(low)), axis=0)
        for weight in (o_weight, gate_weight, up_weight, down_weight)
    )
    rows_chunks = rings.gather(inputs)
    rows_in = jnp.concatenate(rows_chunks, axis=0)

    order = rings.order()
    token_rows = jnp.arange(tok_rows, dtype=jnp.int32)
    positions = ((range_index * groups + order)[:, None] * tok_rows + token_rows[None, :]).reshape(-1)
    frequency = rope_base ** (-(jnp.arange(dim // 2, dtype=full) * 2.0) / dim)
    angles = positions.astype(full)[:, None] * frequency[None, :]
    cosine, sine = (jnp.cos(angles), jnp.sin(angles))
    cos_table = jnp.concatenate([cosine, cosine], axis=1)
    sin_table = jnp.concatenate([-sine, sine], axis=1)
    id_rows = block_ids.reshape(ranges * groups, tok_rows)
    relative = range_index ^ jnp.arange(ranges, dtype=jnp.int32)
    key_ids = id_rows[(relative[:, None] * groups + order[None, :]).reshape(-1)].reshape(-1)
    query_ids = key_ids[:rows_all]
    q_ids = jnp.broadcast_to(query_ids[None, :], (8, rows_all))
    k_ids = key_ids[:, None]

    def limits_of(ids, tile):
        ids = ids.reshape(-1, tile)
        return (jnp.min(ids, axis=1), jnp.max(ids, axis=1))

    q_limits = limits_of(query_ids, q_tile)
    limits = q_limits + limits_of(key_ids, key_tile)
    wide_limits = q_limits + limits_of(key_ids, wide_tile)

    qk_raw = product(rows_in, qkv_full[:, : 2 * cols])
    squares = jnp.stack(
        [jnp.sum(qk_raw[:, i * cols : (i + 1) * cols] ** 2, axis=1) for i in range(2)]
    ).reshape(2, groups, tok_rows)
    placing = (order[None, :] == jnp.arange(groups)[:, None]).astype(full)
    in_true_order = jnp.sum(placing[None, :, :, None] * squares[:, None], axis=2)
    summed = head_sum(in_true_order)
    squares = jnp.sum(placing[None, :, :, None] * summed[:, :, None], axis=1).reshape(2, rows_all)
    scales = lax.rsqrt(squares / width + epsilon).T
    value_raw = product(rows_in, qkv_full[:, 2 * cols :]).astype(low)
    gain_cols = jnp.concatenate([q_gain.T.reshape(cols), k_gain.T.reshape(cols)])
    q_factor = dim**-0.5 / math.log(2.0)
    query_rot, key_rot = prepare(
        qk_raw,
        scales,
        jnp.broadcast_to(gain_cols[None, :], (8, 2 * cols)),
        cos_table,
        sin_table,
        heads,
        dim,
        q_factor,
    )
    values, keys = blk_gather_pair(value_raw, key_rot)
    mixed_low, totals = attend(
        query_rot, keys, values, q_ids, k_ids, wide_limits, heads, dim, q_tile, wide_tile
    )

    attn_own = rings.scatter(
        [
            times_transposed(mixed_low[j * 2 * tok_rows : (j + 1) * 2 * tok_rows], output_full).astype(low)
            for j in range(rings.chips)
        ],
    )
    attn_hat, attn_scale = normalize(attn_own)
    hidden = inputs.astype(full) + attn_hat * attn_gain

    mid_chunks = rings.gather(hidden.astype(low))
    gates, ups, acts, parts = ([], [], [], [])
    for chunk in mid_chunks:
        gate_pre = product(chunk, gate_full)
        up_pre = product(chunk, up_full)
        act = (gate_pre * jax.nn.sigmoid(gate_pre) * up_pre).astype(low)
        gates.append(gate_pre)
        ups.append(up_pre)
        acts.append(act)
        parts.append(times_transposed(act, down_full).astype(low))
    mlp_own = rings.scatter(parts)
    mlp_hat, mlp_scale = normalize(mlp_own)
    result = relative_columns((hidden + mlp_hat * mlp_gain).astype(low))
    grad_out = out_grad.astype(full)
    mlp_gain_part = jnp.sum(grad_out * mlp_hat, axis=0)
    mlp_grad = norm_back(grad_out * mlp_gain, mlp_hat, mlp_scale).astype(low)

    grad_chunks = rings.gather(mlp_grad)
    gate_grads, up_grads, parts = ([], [], [])
    for chunk, gate_pre, up_pre in zip(grad_chunks, gates, ups):
        act_grad = product(chunk, down_full)
        sigmoid_gate = jax.nn.sigmoid(gate_pre)
        gate_grad = (
            act_grad * up_pre * sigmoid_gate * (1.0 + gate_pre * (1.0 - sigmoid_gate))
        ).astype(low)
        up_grad = (act_grad * gate_pre * sigmoid_gate).astype(low)
        gate_grads.append(gate_grad)
        up_grads.append(up_grad)
        parts.append(
            (times_transposed(gate_grad, gate_full) + times_transposed(up_grad, up_full)).astype(low)
        )
    hidden_grad = grad_out + rings.scatter(parts)

    def weight_sum(left, right):
        def part(k):
            return transposed_times(left[:, k * slab : (k + 1) * slab], right)

        return blk_scatter(part)

    rows_mid = jnp.concatenate(mid_chunks, axis=0)
    down_sum = weight_sum(jnp.concatenate(grad_chunks, axis=0), jnp.concatenate(acts, axis=0))
    gate_sum = weight_sum(rows_mid, jnp.concatenate(gate_grads, axis=0))
    up_sum = weight_sum(rows_mid, jnp.concatenate(up_grads, axis=0))
    attn_gain_part = jnp.sum(hidden_grad * attn_hat, axis=0)
    attn_grad = norm_back(hidden_grad * attn_gain, attn_hat, attn_scale).astype(low)
    gain_parts = relative_columns(jnp.stack([attn_gain_part, mlp_gain_part]))
    gain_sums = head_sum(gain_parts.reshape(-1, dim))

    attn_grad_chunks = rings.gather(attn_grad)
    mixed_grad = jnp.concatenate(
        [product(chunk, output_full).astype(low) for chunk in attn_grad_chunks], axis=0
    )
    output_sum = weight_sum(jnp.concatenate(attn_grad_chunks, axis=0), mixed_low)
    query_norm_grads, kv_grads = ([], [])
    for head in range(heads):
        query_norm_grad, *kv_parts = attend_back(
            head,
            query_rot,
            keys,
            values,
            q_ids,
            k_ids,
            limits,
            totals,
            mixed_grad,
            mixed_low,
            cos_table,
            sin_table,
            dim,
            q_tile,
            key_tile,
        )
        query_norm_grads.append(query_norm_grad)
        kv_grads.append(blk_scatter(lambda k, parts=kv_parts: parts[k].astype(full)))

    def over_heads(dots):
        ordered = jnp.sum(placing[:, :, None] * dots.reshape(1, groups, tok_rows), axis=1)
        total = head_sum(ordered)
        return jnp.sum(placing[:, :, None] * total[:, None], axis=0).reshape(rows_all, 1)

    def raw_grads_of(norm_grads, raw, scale, gains):
        weighted, dots, gain_parts = ([], 0.0, [])
        for h, grad in enumerate(norm_grads):
            at = slice(h * dim, (h + 1) * dim)
            product_of = grad * raw[:, at]
            weighted.append(grad * gains[at])
            dots = dots + jnp.sum(product_of * gains[at], axis=1)
            gain_parts.append(jnp.sum(product_of * scale, axis=0))
        dot = over_heads(dots)
        shrink = scale**3 * dot / width
        grads = [
            (scale * w - raw[:, h * dim : (h + 1) * dim] * shrink).astype(low)
            for h, w in enumerate(weighted)
        ]
        return (grads, jnp.stack(gain_parts))

    query_raw_grads, query_gain_part = raw_grads_of(
        query_norm_grads, qk_raw[:, :cols], scales[:, 0:1], gain_cols[:cols]
    )
    key_norm_grads = [unrotate(g[:, :dim], cos_table, sin_table) for g in kv_grads]
    key_raw_grads, key_gain_part = raw_grads_of(
        key_norm_grads, qk_raw[:, cols:], scales[:, 1:2], gain_cols[cols:]
    )
    raw_grads = jnp.concatenate(
        query_raw_grads + key_raw_grads + [g[:, dim:].astype(low) for g in kv_grads], axis=1
    )
    input_grad = relative_columns(
        (
            hidden_grad
            + rings.scatter(
                [
                    times_transposed(
                        raw_grads[j * 2 * tok_rows : (j + 1) * 2 * tok_rows], qkv_full
                    ).astype(low)
                    for j in range(rings.chips)
                ],
            )
        ).astype(low)
    )
    qkv_sum = weight_sum(rows_in, raw_grads)
    small = blk_sum(
        jnp.concatenate([gain_sums, query_gain_part, key_gain_part], axis=0)
    )
    gain_rows = width // dim
    gain_at = range_index * (width // ranges)
    attn_gain_grad = lax.dynamic_slice_in_dim(
        small[:gain_rows].reshape(width), gain_at, width // ranges
    )
    mlp_gain_grad = lax.dynamic_slice_in_dim(
        small[gain_rows : 2 * gain_rows].reshape(width), gain_at, width // ranges
    )
    piece = dim // ranges
    q_gain_grad, k_gain_grad = (
        lax.dynamic_slice_in_dim(
            small[2 * gain_rows + i * heads : 2 * gain_rows + (i + 1) * heads].T,
            range_index * piece,
            piece,
        )
        for i in range(2)
    )
    return (
        result,
        input_grad,
        qkv_sum[:, :cols],
        qkv_sum[:, cols : 2 * cols],
        qkv_sum[:, 2 * cols :],
        output_sum,
        gate_sum,
        up_sum,
        down_sum,
        q_gain_grad,
        k_gain_grad,
        attn_gain_grad,
        mlp_gain_grad,
    )


def solution(mesh):
    in_specs = (
        P(("blk", "head"), None),
        P("blk", "head"),
        P("blk", "head"),
        P("blk", "head"),
        P("blk", "head"),
        P("blk", "head"),
        P("blk", "head"),
        P("blk", "head"),
        P(None, "head"),
        P(None, "head"),
        P(),
        P(),
        P(),
        P(("blk", "head"), None),
    )
    out_specs = (
        P(("blk", "head"), None),
        P(("blk", "head"), None),
        P("blk", "head"),
        P("blk", "head"),
        P("blk", "head"),
        P("blk", "head"),
        P("blk", "head"),
        P("blk", "head"),
        P("blk", "head"),
        P("blk", "head"),
        P("blk", "head"),
        P("blk"),
        P("blk"),
    )
    return jax.shard_map(layer, mesh=mesh, in_specs=in_specs, out_specs=out_specs, check_vma=False)
```
